128 devices in a mesh: req: 16 (over y, x), seq: 8 (over z, core).
Axes of the slice: x: 4, y: 4, z: 4, core: 2. Of those that a mesh axis runs over, the one named last changes fastest.
Arguments:
- qkv_proj: bfloat16 [16, 1024, 4096], P('req', 'seq'), may hold values from -6 to 6
- gate_proj: bfloat16 [16, 1024, 2048], P('req', 'seq'), may hold values from -6 to 6
- residual: bfloat16 [16, 1024, 2048], P('req', 'seq'), may hold values from -6 to 6
- log_decay: float32 [16, 1024, 8], P('req', 'seq'), may hold values from -1 to 0, as said below
- beta_logit: bfloat16 [16, 1024, 8], P('req', 'seq'), may hold values from -6 to 6
- lengths: int32 [16], replicated, may hold values from 1 to 1024, 8192 in all
- slot_request: int32 [16], replicated, may hold values from 0 to 15, each once
- conv_weight: float32 [4, 4096], replicated, may hold values from -3 to 3
- norm_gain: float32 [256], replicated, may hold values from 0.1 to 1.9
- out_weight: bfloat16 [2048, 2048], P(('req', 'seq')), may hold values from -0.125 to 0.125
- mlp_gain: float32 [2048], replicated, may hold values from 0.1 to 1.9
- w_gate: bfloat16 [2048, 5632], P('req', 'seq'), may hold values from -0.125 to 0.125
- w_up: bfloat16 [2048, 5632], P('req', 'seq'), may hold values from -0.125 to 0.125
- w_down: bfloat16 [5632, 2048], P('seq', 'req'), may hold values from -0.078125 to 0.078125
Outputs:
- hidden_out: bfloat16 [16, 1024, 2048], P('req', 'seq')
- final_state: float32 [16, 8, 128, 256], P('req', 'seq')
- conv_edge: bfloat16 [16, 3, 4096], P('req', None, 'seq')
The draws below stay inside these ranges and needn't reach their ends.
Inputs may be any that keep to these rules, and one draw needn't show every extreme that they name: Slot s of the req axis holds request slot_request[s]. The 16 lengths sum to 8192, and the longest is exactly 1024. `log_decay`: every entry is negative.
All inputs are finite; a program needn't handle non-finite values.
Results may differ from the reference program's by a relative error of at most 0.014.
Values may be sent and summed in bfloat16 or wider, within the bound.
A program may use at most 128 MiB of HBM per device.

```python
import math
import jax
import jax.numpy as jnp
import numpy as np
from jax import lax

D = 2048
LOCAL_HEADS = 8
DK = 128
DV = 256
FF = 5632
CONV = 4
PIECE = 128
SLOT_POSITIONS = 1024
REQUEST_COUNT = 16
HK = 1024
HV = 2048
CH = 4096
TOTAL = 8192
N_SEQ = 8


def draw_log_decay(key, part):
    request_lanes = jax.random.split(key, 7)
    slow_share = 0.5
    slow_heads = jax.random.uniform(request_lanes[0], (LOCAL_HEADS,)) < slow_share
    fast_rate = -jnp.exp(jax.random.uniform(request_lanes[1], (LOCAL_HEADS,), minval=math.log(1.0 / 50.0), maxval=math.log(1.0 / 30.0)))
    slow_rate = math.log(0.1) / SLOT_POSITIONS * jax.random.uniform(request_lanes[2], (LOCAL_HEADS,), minval=0.3, maxval=1.0)
    head_decay_speed = jnp.where(slow_heads, slow_rate, fast_rate)
    piece_count = SLOT_POSITIONS // PIECE
    segment_multiplier = jnp.exp2(jax.random.uniform(request_lanes[3], (REQUEST_COUNT, piece_count, 1, LOCAL_HEADS), minval=-0.5, maxval=0.5))
    segment_multiplier = jnp.broadcast_to(segment_multiplier, (REQUEST_COUNT, piece_count, PIECE, LOCAL_HEADS)).reshape(REQUEST_COUNT, SLOT_POSITIONS, LOCAL_HEADS)
    jaggedness = jax.random.uniform(request_lanes[4], (REQUEST_COUNT, SLOT_POSITIONS, LOCAL_HEADS), minval=0.5, maxval=1.5)
    token_clusters = jax.random.uniform(request_lanes[5], (REQUEST_COUNT, SLOT_POSITIONS, LOCAL_HEADS)) < 3.0 / SLOT_POSITIONS
    cluster_length = jnp.log(jax.random.uniform(request_lanes[6], (REQUEST_COUNT, SLOT_POSITIONS, LOCAL_HEADS), minval=0.5, maxval=0.8))
    return (head_decay_speed * segment_multiplier * jaggedness + jnp.where(token_clusters, cluster_length, 0.0)).astype(jnp.float32)


def shard_levels(key, dims, cuts, low, top_value):
    def one(dim, blocks):
        draws = jax.random.uniform(jax.random.fold_in(jax.random.fold_in(key, 6), dim), (blocks,), jnp.float32, low / len(cuts), top_value / len(cuts))
        return jnp.repeat(jnp.exp(draws), dims[dim] // blocks).reshape((-1,) + (1,) * (len(dims) - dim - 1))

    loudness = one(*cuts[0])
    for cut in cuts[1:]:
        loudness = loudness * one(*cut)
    return loudness


def length_profile(amount, total, reach, lean):
    portions = [(1 << 20) // math.isqrt(grade ** lean) + 1 for grade in range(2, amount + 1)]
    rest, holding = total - reach - (amount - 1), [1] * (amount - 1)
    while rest > 0:
        candidates = [i for i in range(amount - 1) if holding[i] < reach]
        mass, left = sum([portions[i] for i in candidates]), rest
        for i in candidates:
            extra = min(reach - holding[i], max(1, left * portions[i] // mass), rest)
            holding[i] = holding[i] + extra
            rest = rest - extra
    return np.array([reach] + holding)


def ragged(stream_key, number_of, total, limit, skew):
    if number_of == 2:
        one = jax.random.randint(stream_key, (), max(1, total - limit), min(limit, total - 1) + 1)
        return jnp.stack([one, total - one])
    tallies = jnp.asarray(length_profile(number_of, total, limit, skew), jnp.int32)
    twos = (number_of - 1) // 2
    source_of, taker = tallies[1:1 + 2 * twos:2], tallies[2:2 + 2 * twos:2]
    margin = jnp.minimum(source_of - 1, limit - taker)
    passed = jax.random.randint(jax.random.fold_in(stream_key, 1), (twos,), 0, 1 << 20) % (margin + 1)
    tallies = tallies.at[1:1 + 2 * twos:2].set(source_of - passed).at[2:2 + 2 * twos:2].set(taker + passed)
    return tallies[jax.random.permutation(jax.random.fold_in(stream_key, 2), number_of)]


def gaussian(rng, shape, scale, most, cuts=(), held_as=jnp.bfloat16):
    loudness = shard_levels(rng, shape, cuts, -0.22, 0.18) if cuts else 1.0
    entries = jax.random.normal(rng, shape, jnp.float32) * scale * loudness
    return jnp.minimum(jnp.maximum(entries, -most), most).astype(held_as)


def setup_inputs(seed: int = 0) -> dict:
    arg_keys = jax.random.split(jax.random.key(seed), 15)
    return {
        "qkv_proj": gaussian(arg_keys[0], (REQUEST_COUNT, SLOT_POSITIONS, CH), 1.0, 6.0, ((0, 16), (1, 8))),
        "gate_proj": gaussian(arg_keys[1], (REQUEST_COUNT, SLOT_POSITIONS, HV), 1.0, 6.0, ((0, 16), (1, 8))),
        "residual": gaussian(arg_keys[2], (REQUEST_COUNT, SLOT_POSITIONS, D), 1.0, 6.0, ((0, 16), (1, 8))),
        "log_decay": draw_log_decay(jax.random.fold_in(arg_keys[14], 71), 0),
        "beta_logit": gaussian(arg_keys[4], (REQUEST_COUNT, SLOT_POSITIONS, LOCAL_HEADS), 1.5, 6.0, ((0, 16), (1, 8))),
        "lengths": ragged(arg_keys[5], REQUEST_COUNT, TOTAL, SLOT_POSITIONS, 2).astype(jnp.int32),
        "slot_request": jax.random.permutation(arg_keys[6], REQUEST_COUNT).astype(jnp.int32),
        "conv_weight": gaussian(arg_keys[7], (CONV, CH), 0.5, 3.0, (), jnp.float32),
        "norm_gain": jnp.clip(1.0 + 0.18 * jax.random.normal(arg_keys[8], (DV,), jnp.float32), 0.1, 1.9),
        "out_weight": gaussian(arg_keys[9], (HV, D), HV ** -0.5, 0.125, ((0, 128),)),
        "mlp_gain": jnp.clip(1.0 + 0.18 * jax.random.normal(arg_keys[10], (D,), jnp.float32), 0.1, 1.9),
        "w_gate": gaussian(arg_keys[11], (D, FF), D ** -0.5, 0.125, ((0, 16), (1, 8))),
        "w_up": gaussian(arg_keys[12], (D, FF), D ** -0.5, 0.125, ((0, 16), (1, 8))),
        "w_down": gaussian(arg_keys[13], (FF, D), FF ** -0.5, 0.078125, ((0, 8), (1, 16))),
    }


EPS_NORM = 1e-05
EPS_UNIT = 1e-06
HIGHEST = lax.Precision.HIGHEST

def unit_norm(vector):
    return vector * lax.rsqrt(lax.optimization_barrier(jnp.sum(vector * vector, axis=-1, keepdims=True)) + EPS_UNIT)

def reference(qkv_proj, gate_proj, residual, log_decay, beta_logit, lengths, slot_request, conv_weight, norm_gain, out_weight, mlp_gain, w_gate, w_up, w_down):
    slot_length = jnp.take(lengths, slot_request)
    position = jnp.arange(SLOT_POSITIONS, dtype=jnp.int32)
    live_mask = position[None, :] < slot_length[:, None]
    inputs = qkv_proj.astype(jnp.float32)
    padded = jnp.pad(inputs, ((0, 0), (CONV - 1, 0), (0, 0)))
    convolved = jnp.zeros_like(inputs)
    for offset in range(CONV):
        convolved = convolved + conv_weight[offset] * padded[:, offset:offset + SLOT_POSITIONS]
    activated = jax.nn.silu(convolved)
    query_vec = unit_norm(activated[..., :HK].reshape(REQUEST_COUNT, SLOT_POSITIONS, LOCAL_HEADS, DK)) * DK ** (-0.5)
    key_vecs = unit_norm(activated[..., HK:2 * HK].reshape(REQUEST_COUNT, SLOT_POSITIONS, LOCAL_HEADS, DK))
    values = activated[..., 2 * HK:].reshape(REQUEST_COUNT, SLOT_POSITIONS, LOCAL_HEADS, DV)
    beta_gate = jax.nn.sigmoid(beta_logit.astype(jnp.float32)) * live_mask[..., None]
    decay_rate = jnp.exp(jnp.where(live_mask[..., None], log_decay, 0.0))

    def advance(carry_state, inputs_now):
        query_now, keys_now, values_now, beta_now, decay_now = inputs_now
        projected = jnp.einsum('rhk,rhkv->rhv', keys_now, carry_state, precision=HIGHEST)
        rank_one = beta_now[..., None, None] * keys_now[..., :, None]
        carry_state = decay_now[..., None, None] * (carry_state - rank_one * projected[..., None, :]) + rank_one * values_now[..., None, :]
        output_now = jnp.einsum('rhk,rhkv->rhv', query_now, carry_state, precision=HIGHEST)
        return (carry_state, output_now)
    sequence = tuple((jnp.moveaxis(tensor, 1, 0) for tensor in (query_vec, key_vecs, values, beta_gate, decay_rate)))
    initial = jnp.zeros((REQUEST_COUNT, LOCAL_HEADS, DK, DV), jnp.float32)
    final_state, outputs = lax.scan(advance, initial, sequence)
    outputs = jnp.moveaxis(outputs, 0, 1)
    edge_index = slot_length[:, None] - (CONV - 1) + jnp.arange(CONV - 1, dtype=jnp.int32)[None, :]
    taken = jnp.take_along_axis(qkv_proj, jnp.clip(edge_index, 0, SLOT_POSITIONS - 1)[:, :, None], axis=1)
    conv_edge = jnp.where((edge_index >= 0)[:, :, None], taken, jnp.zeros_like(taken))
    gate_values = gate_proj.astype(jnp.float32).reshape(REQUEST_COUNT, SLOT_POSITIONS, LOCAL_HEADS, DV)
    scaled = outputs * lax.rsqrt(lax.optimization_barrier(jnp.mean(outputs * outputs, axis=-1, keepdims=True)) + EPS_NORM)
    mixed_heads = (scaled * norm_gain * jax.nn.silu(gate_values)).reshape(REQUEST_COUNT, SLOT_POSITIONS, HV).astype(jnp.bfloat16)
    shard_width = FF // N_SEQ

    def finish(request_items):
        mixed_rows, residual_rows, live_rows = request_items
        attended = jnp.dot(mixed_rows, out_weight, preferred_element_type=jnp.float32)
        hidden_state = (residual_rows.astype(jnp.float32) + attended).astype(jnp.bfloat16)
        stream = hidden_state.astype(jnp.float32)
        normed = (stream * lax.rsqrt(lax.optimization_barrier(jnp.mean(stream * stream, axis=-1, keepdims=True)) + EPS_NORM) * mlp_gain).astype(jnp.bfloat16)
        gate_part = jnp.dot(normed, w_gate, preferred_element_type=jnp.float32)
        upward = jnp.dot(normed, w_up, preferred_element_type=jnp.float32)
        inner_units = (jax.nn.silu(gate_part) * upward).astype(jnp.bfloat16)
        combined = stream
        for shard_index in range(N_SEQ):
            lower_edge = shard_index * shard_width
            partial_value = jnp.dot(inner_units[:, lower_edge:lower_edge + shard_width], w_down[lower_edge:lower_edge + shard_width], preferred_element_type=jnp.float32)
            combined = combined + lax.optimization_barrier(partial_value.astype(jnp.bfloat16)).astype(jnp.float32)
        return jnp.where(live_rows[:, None], combined, 0.0).astype(jnp.bfloat16)
    hidden_out = lax.map(finish, (mixed_heads, residual, live_mask))
    return (hidden_out, final_state, conv_edge)
```

```python
import functools

import jax
import jax.numpy as jnp
from jax import lax
from jax.experimental import pallas as pl
from jax.experimental.pallas import tpu as pltpu
from jax.sharding import PartitionSpec as P

MESH = pl.DeviceIdType.MESH
BF = jnp.bfloat16
F32 = jnp.float32

HEADS = 8
DK = 128
DV = 256
CONV = 4
HK = 1024
PIECE = 128
D = 2048
UNITS = 704
HALF = UNITS // 2
PAD = 16
EPS_NORM = 1e-05
EPS_UNIT = 1e-06


def dot(a, b):
    return jnp.dot(a, b, preferred_element_type=F32)


def dot_nt(a, b):
    return lax.dot_general(a, b, (((1,), (1,)), ((), ())), preferred_element_type=F32)


def parts(a):
    high = a.astype(BF)
    return high, (a - high.astype(F32)).astype(BF)


def left3(a):
    high, low = parts(a)
    return jnp.concatenate([high, high, low], axis=1)


def right3(a, axis=0):
    high, low = parts(a)
    return jnp.concatenate([high, low, high], axis=axis)


def silu(v):
    return v / (1.0 + jnp.exp(-v))


class Copies:
    def __init__(self, send, recv):
        self.send, self.recv, self.used, self.sent = send, recv, 0, []

    def take(self):
        self.used += 1
        return self.used - 1

    def start(self, index, view, device, own=None):
        src, dst = (own if own is not None else view()), view()
        copy = pltpu.make_async_remote_copy(
            src_ref=src,
            dst_ref=dst,
            send_sem=self.send.at[index],
            recv_sem=self.recv.at[index],
            device_id=device,
            device_id_type=MESH,
        )
        copy.start()
        self.sent.append((index, view, device))

    def arrived(self, index, dst, device):
        pltpu.make_async_remote_copy(
            src_ref=dst,
            dst_ref=dst,
            send_sem=self.send.at[index],
            recv_sem=self.recv.at[index],
            device_id=device,
            device_id_type=MESH,
        ).wait_recv()

    def drain(self):
        for index, view, device in self.sent:
            src = dst = view()
            pltpu.make_async_remote_copy(
                src_ref=src,
                dst_ref=dst,
                send_sem=self.send.at[index],
                recv_sem=self.recv.at[index],
                device_id=device,
                device_id_type=MESH,
            ).wait_send()
        self.sent = []


class Ring:
    def __init__(self, copies, me, plus, minus, items):
        self.copies, self.me, self.plus, self.minus = copies, me, plus, minus
        self.items = [(own, slot, half, [copies.take() for _ in range(4)]) for own, slot, half in items]
        self.left, self.right, self.far = (lax.rem(me + step, 4) for step in (3, 1, 2))

    def first(self):
        for own, slot, half, sems in self.items:
            view = functools.partial(slot, self.me)
            self.copies.start(sems[0], view, self.plus, own)
            self.copies.start(sems[1], view, self.minus, own)

    def second(self):
        for own, slot, half, sems in self.items:
            left, right = self.left, self.right
            self.copies.arrived(sems[0], slot(left), self.plus)
            self.copies.start(sems[2], functools.partial(half, left, 0), self.plus)
            self.copies.arrived(sems[1], slot(right), self.minus)
            self.copies.start(sems[3], functools.partial(half, right, 1), self.minus)

    def last(self):
        for own, slot, half, sems in self.items:
            far = self.far
            self.copies.arrived(sems[2], half(far, 0), self.plus)
            self.copies.arrived(sems[3], half(far, 1), self.minus)


def body(
    qkv, edge_in, gb_in, gate_in, res_in, out_w, w_gate, w_up, w_down,
    live, conv_w, norm_gain, mlp_gain,
    hidden, state_out, edge_out,
    kbuf, vbuf, qbuf, gbuf, ebuf,
    x3, kn_s, tv_s, tk_s, kd_s, a_s, qe_s, dec_s, w_s,
    obuf, mixed, gate, resid, stream,
    ow, wg, wu, wd, tok,
    hbuf, pown, psib, prec, s2, sn, r2, rn,
    send, recv, asend, arecv, bsend, brecv, local,
):
    req = lax.axis_index("req")
    seq = lax.axis_index("seq")
    y, x = lax.div(req, 4), lax.rem(req, 4)
    z, c = lax.div(seq, 2), lax.rem(seq, 2)
    other = 1 - c

    def up(v):
        return lax.rem(v + 1, 4)

    def down(v):
        return lax.rem(v + 3, 4)

    xu, xd, xf = up(x), down(x), lax.rem(x + 2, 4)
    yu, yd, yf = up(y), down(y), lax.rem(y + 2, 4)
    zu, zd, zf = up(z), down(z), lax.rem(z + 2, 4)
    xp, xm = (y * 4 + up(x), seq), (y * 4 + down(x), seq)
    yp, ym = (up(y) * 4 + x, seq), (down(y) * 4 + x, seq)
    zp, zm = (req, up(z) * 2 + c), (req, down(z) * 2 + c)
    sib = (req, z * 2 + other)

    barrier = pltpu.get_barrier_semaphore()
    for dev in (xp, xm, yp, ym):
        pl.semaphore_signal(barrier, inc=1, device_id=dev, device_id_type=MESH)
    for step in range(1, 8):
        pl.semaphore_signal(
            barrier, inc=1, device_id=(req, lax.rem(seq + step, 8)), device_id_type=MESH
        )

    def near(index, src, dst):
        return pltpu.make_async_copy(src, dst, local.at[index])

    qcol = pl.multiple_of(seq * DK, DK)
    kcol = pl.multiple_of(HK + seq * DK, DK)
    vcol = pl.multiple_of(2 * HK + seq * DV, DV)
    mine = pl.ds(pl.multiple_of(PAD + seq * PIECE, 16), PIECE)
    locals_ = [
        near(0, gb_in.at[seq], gbuf.at[seq]),
        near(1, qkv.at[:, pl.ds(kcol, DK)], kbuf.at[mine]),
        near(2, qkv.at[:, pl.ds(vcol, DV)], vbuf.at[mine]),
        near(3, qkv.at[:, pl.ds(qcol, DK)], qbuf.at[mine]),
        near(4, edge_in.at[seq], ebuf.at[seq]),
        near(5, gate_in, gate),
        near(6, res_in, resid),
        near(7, out_w, ow.at[y, x, z, c]),
        near(8, w_gate, wg.at[y, x]),
        near(9, w_up, wu.at[y, x]),
        near(10, w_down, wd.at[y, x]),
    ]
    for copy in locals_:
        copy.start()
    for buf in (kbuf, vbuf, qbuf):
        buf[0:PAD, :] = jnp.zeros((PAD, buf.shape[1]), BF)
    pl.semaphore_wait(barrier, 11)

    copies = Copies(send, recv)

    def cut(ref, first, size):
        return ref.at[pl.ds(first, size)]

    ring_oz = Ring(copies, z, zp, zm, [(
        out_w,
        lambda i: ow.at[y, x, i, c],
        lambda i, h: ow.at[y, x, i, c, :, h * 1024 : h * 1024 + 1024],
    )])
    ring_wax = Ring(copies, x, xp, xm, [
        (w_gate, lambda i: wg.at[y, i], lambda i, h: wg.at[y, i, h * 64 : h * 64 + 64]),
        (
            w_down.at[0:HALF],
            lambda i: wd.at[y, i, 0:HALF],
            lambda i, h: wd.at[y, i, h * 176 : h * 176 + 176],
        ),
    ])
    ring_wby = Ring(copies, y, yp, ym, [
        (w_up, lambda i: wu.at[i, x], lambda i, h: wu.at[i, x, h * 64 : h * 64 + 64]),
        (
            w_down.at[HALF:UNITS],
            lambda i: wd.at[i, x, HALF:UNITS],
            lambda i, h: wd.at[i, x, HALF + h * 176 : HALF + h * 176 + 176],
        ),
    ])
    ring_way = Ring(copies, y, yp, ym, [
        (None, lambda i: wg.at[i], lambda i, h: wg.at[i, 2 * h : 2 * h + 2]),
        (None, lambda i: wd.at[i, :, 0:HALF], lambda i, h: wd.at[i, 2 * h : 2 * h + 2, 0:HALF]),
    ])
    ring_wbx = Ring(copies, x, xp, xm, [
        (None, lambda i: wu.at[:, i], lambda i, h: wu.at[2 * h : 2 * h + 2, i]),
        (
            None,
            lambda i: wd.at[:, i, HALF:UNITS],
            lambda i, h: wd.at[2 * h : 2 * h + 2, i, HALF:UNITS],
        ),
    ])
    lo, hi = slice(0, 1024), slice(1024, 2048)
    ring_o1x = Ring(copies, x, xp, xm, [(
        None,
        lambda i: ow.at[y, i, :, c, :, lo],
        lambda i, h: ow.at[y, i, 2 * h : 2 * h + 2, c, :, lo],
    )])
    ring_o2y = Ring(copies, y, yp, ym, [(
        None,
        lambda i: ow.at[i, x, :, c, :, hi],
        lambda i, h: ow.at[i, x, 2 * h : 2 * h + 2, c, :, hi],
    )])
    ring_o1y = Ring(copies, y, yp, ym, [(
        None,
        lambda i: ow.at[i, :, :, c, :, lo],
        lambda i, h: ow.at[i, 2 * h : 2 * h + 2, :, c, :, lo],
    )])
    ring_o2x = Ring(copies, x, xp, xm, [(
        None,
        lambda i: ow.at[:, i, :, c, :, hi],
        lambda i, h: ow.at[2 * h : 2 * h + 2, i, :, c, :, hi],
    )])
    ring_tok = Ring(copies, z, zp, zm, [(
        None,
        lambda i: tok.at[i, c],
        lambda i, h: tok.at[i, c, h * 64 : h * 64 + 64],
    )])

    def exchange(kind, src, dst, dev, peer):
        return pltpu.make_async_remote_copy(
            src_ref=src, dst_ref=dst, send_sem=asend.at[kind, peer], recv_sem=arecv.at[kind, seq],
            device_id=dev, device_id_type=MESH,
        )

    def views(kind, head, piece):
        rows = pl.ds(pl.multiple_of(PAD + piece * PIECE, 16), PIECE)
        if kind == 0:
            return gb_in.at[head], gbuf.at[piece]
        if kind == 1:
            return qkv.at[:, pl.ds(pl.multiple_of(HK + head * DK, DK), DK)], kbuf.at[rows]
        if kind == 2:
            return qkv.at[:, pl.ds(pl.multiple_of(2 * HK + head * DV, DV), DV)], vbuf.at[rows]
        if kind == 3:
            return qkv.at[:, pl.ds(pl.multiple_of(head * DK, DK), DK)], qbuf.at[rows]
        return edge_in.at[head], ebuf.at[piece]

    order = (4, 3, 5, 2, 6, 7, 1)

    def spread(kind):
        for step in order:
            peer = lax.rem(seq + step, 8)
            src, dst = views(kind, peer, seq)
            exchange(kind, src, dst, (req, peer), peer).start()

    def piece_arrived(kind, piece):
        @pl.when(piece != seq)
        def _():
            src, dst = views(kind, seq, piece)
            pltpu.make_async_remote_copy(
                src_ref=dst, dst_ref=dst, send_sem=asend.at[kind, piece],
                recv_sem=arecv.at[kind, piece], device_id=(req, piece), device_id_type=MESH,
            ).wait_recv()

    ring_oz.first()
    spread(0)
    spread(1)
    ring_wax.first()
    ring_wby.first()
    ring_oz.second()
    spread(2)
    spread(3)
    spread(4)
    for index in range(4):
        locals_[index].wait()

    row = lax.broadcasted_iota(jnp.int32, (PIECE, PIECE), 0)
    col = lax.broadcasted_iota(jnp.int32, (PIECE, PIECE), 1)

    def convolve(buf, piece, taps):
        window = buf[pl.ds(pl.multiple_of(piece * PIECE, 16), PAD + PIECE), :].astype(F32)
        total = window[PAD:] * taps[CONV - 1 : CONV]
        for tap in range(CONV - 1):
            total = total + pltpu.roll(window, CONV - 1 - tap, 0)[PAD:] * taps[tap : tap + 1]
        return silu(total)

    def unit(v):
        return v * lax.rsqrt(jnp.sum(v * v, axis=-1, keepdims=True) + EPS_UNIT)

    def gates(piece):
        tile = gbuf[piece]
        log_row, beta_row = tile[0:1], tile[1:2]
        grown = jnp.sum(jnp.where(col <= row, log_row, 0.0), axis=1, keepdims=True)
        beta = jnp.sum(jnp.where(col == row, beta_row, 0.0), axis=1, keepdims=True)
        return log_row, grown, beta

    ktaps = conv_w[:, pl.ds(kcol, DK)]
    vtaps = conv_w[:, pl.ds(vcol, DV)]
    qtaps = conv_w[:, pl.ds(qcol, DK)]
    eye = jnp.where(row == col, 1.0, 0.0).astype(F32)

    GROUP = 4

    def invert(step, carry):
        pieces = [step * GROUP + j for j in range(GROUP)]
        for piece in pieces:
            piece_arrived(0, piece)
            piece_arrived(1, piece)
        couples, inverses = [], []
        for piece in pieces:
            key = unit(convolve(kbuf, piece, ktaps))
            kn_s[piece] = key
            log_row, grown, beta = gates(piece)
            log_col = jnp.sum(jnp.where(col == row, log_row, 0.0), axis=1, keepdims=True)
            along = jnp.sum(jnp.where(row <= col, log_col, 0.0), axis=0, keepdims=True)
            within = jnp.where(col <= row, jnp.exp(jnp.minimum(grown - along, 0.0)), 0.0)
            w_s[piece] = within
            inner = dot_nt(left3(key), right3(key, 1))
            couple = jnp.where(col < row, beta * within * inner, 0.0)
            couples.append(couple)
            inverses.append(eye - jnp.where((row // 2) == (col // 2), couple, 0.0))
        size = 2
        while size < PIECE:
            mask = ((row // (2 * size)) == (col // (2 * size))) & ((row // size) != (col // size))
            lows = [v.astype(BF) for v in inverses]
            mids = [
                dot(low, jnp.where(mask, couple, 0.0).astype(BF)).astype(BF)
                for low, couple in zip(lows, couples)
            ]
            inverses = [v - dot(mid, low) for v, mid, low in zip(inverses, mids, lows)]
            size *= 2
        rests = [
            eye - v - dot(left3(couple), right3(v)) for v, couple in zip(inverses, couples)
        ]
        for piece, v, rest in zip(pieces, inverses, rests):
            x3[piece] = left3(v + dot(v.astype(BF), rest.astype(BF)))

        @pl.when(step == 0)
        def _():
            ring_oz.last()
            locals_[7].wait()
            ring_o1x.first()
            ring_o2y.first()

        return carry

    lax.fori_loop(0, HEADS // GROUP, invert, 0)
    ring_wax.second()
    ring_wby.second()
    ring_o1x.second()
    ring_o2y.second()

    def prepare(step, carry):
        pieces = [step * 2 + j for j in range(2)]
        for piece in pieces:
            piece_arrived(2, piece)
            piece_arrived(3, piece)
        for piece in pieces:
            query = unit(convolve(qbuf, piece, qtaps)) * DK ** (-0.5)
            value = convolve(vbuf, piece, vtaps)
            key = kn_s[piece]
            log_row, grown, beta = gates(piece)
            whole = jnp.sum(log_row, axis=1, keepdims=True)
            growth = jnp.exp(grown)
            a_s[piece] = (w_s[piece] * dot_nt(left3(query), right3(key, 1))).astype(BF)
            qe_s[piece] = (growth * query).astype(BF)
            both = jnp.concatenate([beta * value, (beta * growth) * key], axis=1)
            solved = dot(x3[piece], right3(both))
            tv_s[piece] = solved[:, :DV]
            tk_s[piece] = left3(solved[:, DV:])
            kd_s[piece] = left3(jnp.transpose(jnp.exp(jnp.minimum(whole - grown, 0.0)) * key))
            dec_s[piece] = jnp.broadcast_to(jnp.exp(whole), (8, DV))

        return carry

    lax.fori_loop(0, HEADS // 2, prepare, 0)

    ring_o1x.last()
    ring_o2y.last()
    forwards = [copies.take() for _ in range(8)]

    def forward_o(first, index):
        copies.start(forwards[first], lambda: ow.at[index[0], :, :, c, :, lo], sib)
        copies.start(forwards[first + 1], lambda: ow.at[:, index[1], :, c, :, hi], sib)

    ring_o1y.first()
    ring_o2x.first()
    forward_o(0, (y, x))

    state_out[...] = jnp.zeros((DK, DV), F32)

    def back(piece):
        return pltpu.make_async_remote_copy(
            src_ref=obuf.at[piece], dst_ref=mixed.at[seq], send_sem=bsend.at[piece],
            recv_sem=brecv.at[seq], device_id=(req, piece), device_id_type=MESH,
        )

    def serial(piece, carry):
        running = state_out[...]
        corrected = tv_s[piece] - dot(tk_s[piece], right3(running))
        result = dot(qe_s[piece], running.astype(BF)) + dot(a_s[piece], corrected.astype(BF))
        state_out[...] = dec_s[piece][0:1] * running + dot(kd_s[piece], right3(corrected))
        scaled = result * lax.rsqrt(jnp.mean(result * result, axis=-1, keepdims=True) + EPS_NORM)

        @pl.when(piece == seq)
        def _():
            mixed[seq] = scaled.astype(BF)

        @pl.when(piece != seq)
        def _():
            obuf[piece] = scaled.astype(BF)
            back(piece).start()

        @pl.when(piece == 3)
        def _():
            ring_o1y.second()
            ring_o2x.second()
            forward_o(2, (yd, xd))
            forward_o(4, (yu, xu))

        return carry

    lax.fori_loop(0, HEADS, serial, 0)

    ring_wax.last()
    ring_wby.last()
    for index in (5, 6, 8, 9, 10):
        locals_[index].wait()
    ring_way.first()
    ring_wbx.first()

    ring_o1y.last()
    ring_o2x.last()
    forward_o(6, (yf, xf))

    for head in range(HEADS):
        @pl.when(head != seq)
        def _():
            pltpu.make_async_remote_copy(
                src_ref=mixed.at[head], dst_ref=mixed.at[head], send_sem=bsend.at[head],
                recv_sem=brecv.at[head], device_id=(req, head), device_id_type=MESH,
            ).wait_recv()

    gain = norm_gain[...]

    def gated(head, carry):
        columns = pl.ds(pl.multiple_of(head * DV, DV), DV)
        value = silu(gate[:, columns].astype(F32)) * gain
        mixed[head] = (mixed[head].astype(F32) * value).astype(BF)
        return carry

    lax.fori_loop(0, HEADS, gated, 0)

    for first, pair in ((0, (y, x)), (2, (yd, xd)), (4, (yu, xu)),
                        (6, (yf, xf))):
        copies.arrived(forwards[first], ow.at[pair[0], :, :, other, :, lo], sib)
        copies.arrived(forwards[first + 1], ow.at[:, pair[1], :, other, :, hi], sib)

    def project(tile, squares):
        columns = pl.ds(pl.multiple_of(tile * 256, 256), 256)
        attended = jnp.zeros((PIECE, 256), F32)
        for head in range(HEADS):
            rows = ow[head // 2, 2 * (head % 2) : 2 * (head % 2) + 2, :, :, :, columns]
            attended = attended + dot(mixed[head], rows.reshape(DV, 256))
        summed = (resid[:, columns].astype(F32) + attended).astype(BF)
        stream[:, columns] = summed
        wide = summed.astype(F32)
        return squares + jnp.sum(wide * wide, axis=-1, keepdims=True)

    squares = lax.fori_loop(0, D // 256, project, jnp.zeros((PIECE, 1), F32))
    scale = lax.rsqrt(squares * (1.0 / D) + EPS_NORM)
    tok[z, c] = (stream[...].astype(F32) * scale * mlp_gain[...]).astype(BF)

    tok_forward = [copies.take() for _ in range(4)]
    ring_tok.first()

    def forward_tok(index, zi):
        copies.start(tok_forward[index], lambda: tok.at[zi, c], sib)

    forward_tok(0, z)
    ring_tok.second()
    forward_tok(1, zd)
    forward_tok(2, zu)

    ring_way.second()
    ring_wbx.second()
    ring_tok.last()
    forward_tok(3, zf)
    for index, zi in ((0, z), (1, zd), (2, zu), (3, zf)):
        copies.arrived(tok_forward[index], tok.at[zi, other], sib)
    ring_way.last()
    ring_wbx.last()

    half_ids = [copies.take() for _ in range(4)]

    def cross(zi):
        return pltpu.make_async_remote_copy(
            src_ref=psib.at[zi], dst_ref=prec.at[zi], send_sem=bsend.at[8 + zi],
            recv_sem=brecv.at[8 + zi], device_id=sib, device_id_type=MESH,
        )

    def paired(zi):
        cross(zi).wait_recv()
        return pown[zi] + prec[zi].astype(F32)

    def far_sum():
        s2[...] = paired(zf).astype(BF)
        copies.start(half_ids[0], lambda: r2.at[0], zp, s2.at[0:64])
        copies.start(half_ids[1], lambda: r2.at[1], zm, s2.at[64:128])

    def next_sum(index):
        total = paired(zu if index == 0 else zd)
        copies.arrived(half_ids[index], r2.at[index], zp if index == 0 else zm)
        other_half = r2[index].astype(F32)
        if index == 0:
            sn[0, 0:64] = (total[0:64] + other_half).astype(BF)
            sn[0, 64:128] = total[64:128].astype(BF)
        else:
            sn[1, 0:64] = total[0:64].astype(BF)
            sn[1, 64:128] = (total[64:128] + other_half).astype(BF)
        copies.start(half_ids[2 + index], lambda: rn.at[index], zp if index == 0 else zm, sn.at[index])

    def ffn(step, carry):
        zi = (z + 10 - (step * (step + 1)) // 2) % 4
        tokens = jnp.concatenate([tok[zi, c], tok[zi, other]], axis=0)
        for first, width in ((0, 256), (256, 256), (512, 192)):
            gate_w = wg[:, :, :, first : first + width].reshape(D, width)
            up_w = wu[:, :, :, first : first + width].reshape(D, width)
            inner = silu(dot(tokens, gate_w)) * dot(tokens, up_w)
            hbuf[:, first : first + width] = inner.astype(BF)

        def lower(tile, carry):
            yi, xi = tile // 2, 2 * (tile % 2)
            rows = jnp.concatenate([wd[yi, xi], wd[yi, xi + 1]], axis=1)
            result = dot(hbuf[...], rows)
            columns = pl.ds(pl.multiple_of(tile * 256, 256), 256)
            pown[zi, :, columns] = result[:PIECE]
            psib[zi, :, columns] = result[PIECE:].astype(BF)
            return carry

        lax.fori_loop(0, D // 256, lower, 0)
        cross(zi).start()

        @pl.when(step == 1)
        def _():
            far_sum()

        @pl.when(step == 2)
        def _():
            next_sum(0)

        @pl.when(step == 3)
        def _():
            next_sum(1)

        return carry

    lax.fori_loop(0, 4, ffn, 0)

    total = stream[...].astype(F32) + paired(z)
    copies.arrived(half_ids[2], rn.at[0], zp)
    copies.arrived(half_ids[3], rn.at[1], zm)
    total = total + rn[0].astype(F32) + rn[1].astype(F32)
    hidden[...] = (total * live[...]).astype(BF)

    for piece in range(HEADS):
        piece_arrived(4, piece)
    locals_[4].wait()
    edges = ebuf[0].astype(F32)
    for piece in range(1, HEADS):
        edges = edges + ebuf[piece].astype(F32)
    edge_out[...] = edges.astype(BF)

    copies.drain()
    for kind in range(5):
        for step in order:
            peer = lax.rem(seq + step, 8)
            src, dst = views(kind, peer, seq)
            exchange(kind, src, dst, (req, peer), peer).wait_send()
    for step in range(1, 8):
        back(lax.rem(seq + step, 8)).wait_send()
    for zi in range(4):
        cross(zi).wait_send()


def layer(qkv, edge, gb, gate, residual, out_weight, w_gate, w_up, w_down, live, conv_weight, norm_gain, mlp_gain):
    hbm = pl.BlockSpec(memory_space=pl.ANY)
    vmem = pl.BlockSpec(memory_space=pltpu.VMEM)
    n_sems = 96
    scratch = [
        pltpu.VMEM((PAD + 1024, DK), BF),
        pltpu.VMEM((PAD + 1024, DV), BF),
        pltpu.VMEM((PAD + 1024, DK), BF),
        pltpu.VMEM((8, 8, 128), F32),
        pltpu.VMEM((8, 16, 512), BF),
        pltpu.VMEM((8, 128, 384), BF),
        pltpu.VMEM((8, 128, 128), F32),
        pltpu.VMEM((8, 128, 256), F32),
        pltpu.VMEM((8, 128, 384), BF),
        pltpu.VMEM((8, 128, 384), BF),
        pltpu.VMEM((8, 128, 128), BF),
        pltpu.VMEM((8, 128, 128), BF),
        pltpu.VMEM((8, 8, 256), F32),
        pltpu.VMEM((8, 128, 128), F32),
        pltpu.VMEM((8, 128, 256), BF),
        pltpu.VMEM((8, 128, 256), BF),
        pltpu.VMEM((128, 2048), BF),
        pltpu.VMEM((128, 2048), BF),
        pltpu.VMEM((128, 2048), BF),
        pltpu.VMEM((4, 4, 4, 2, 16, 2048), BF),
        pltpu.VMEM((4, 4, 128, UNITS), BF),
        pltpu.VMEM((4, 4, 128, UNITS), BF),
        pltpu.VMEM((4, 4, UNITS, 128), BF),
        pltpu.VMEM((4, 2, 128, 2048), BF),
        pltpu.VMEM((256, UNITS), BF),
        pltpu.VMEM((4, 128, 2048), F32),
        pltpu.VMEM((4, 128, 2048), BF),
        pltpu.VMEM((4, 128, 2048), BF),
        pltpu.VMEM((128, 2048), BF),
        pltpu.VMEM((2, 128, 2048), BF),
        pltpu.VMEM((2, 64, 2048), BF),
        pltpu.VMEM((2, 128, 2048), BF),
        pltpu.SemaphoreType.DMA((n_sems,)),
        pltpu.SemaphoreType.DMA((n_sems,)),
        pltpu.SemaphoreType.DMA((5, 8)),
        pltpu.SemaphoreType.DMA((5, 8)),
        pltpu.SemaphoreType.DMA((12,)),
        pltpu.SemaphoreType.DMA((12,)),
        pltpu.SemaphoreType.DMA((11,)),
    ]
    return pl.pallas_call(
        body,
        out_shape=(
            jax.ShapeDtypeStruct((PIECE, D), BF),
            jax.ShapeDtypeStruct((DK, DV), F32),
            jax.ShapeDtypeStruct((16, 512), BF),
        ),
        in_specs=[hbm] * 9 + [vmem] * 4,
        out_specs=(vmem, vmem, vmem),
        scratch_shapes=scratch,
        compiler_params=pltpu.CompilerParams(
            collective_id=0, has_side_effects=True, vmem_limit_bytes=64_000_000
        ),
        name="layer",
    )(qkv, edge, gb, gate, residual, out_weight, w_gate, w_up, w_down, live, conv_weight, norm_gain, mlp_gain)


def local_step(
    qkv_proj, gate_proj, residual, log_decay, beta_logit, lengths, slot_request, conv_weight,
    norm_gain, out_weight, mlp_gain, w_gate, w_up, w_down,
):
    seq_index = lax.axis_index("seq")
    req_index = lax.axis_index("req")
    ids = jnp.arange(slot_request.shape[0], dtype=jnp.int32)
    request = jnp.sum(jnp.where(ids == req_index, slot_request, 0))
    length = jnp.sum(jnp.where(ids == request, lengths, 0))
    position = seq_index * PIECE + jnp.arange(PIECE, dtype=jnp.int32)
    live = position < length
    beta = jax.nn.sigmoid(beta_logit[0].astype(F32)) * live[:, None]
    decay = jnp.where(live[:, None], log_decay[0], 0.0)
    gb = jnp.concatenate(
        [decay.T[:, None], beta.T[:, None], jnp.zeros((HEADS, 6, PIECE), F32)], axis=1
    )
    targets = length - (CONV - 1) + jnp.arange(16, dtype=jnp.int32)
    select = (position[None, :] == targets[:, None]) & (jnp.arange(16)[:, None] < CONV - 1)
    edge = jnp.dot(select.astype(BF), qkv_proj[0], preferred_element_type=F32).astype(BF)
    edge = edge.reshape(16, 8, 512).transpose(1, 0, 2)
    hidden, state, edges = layer(
        qkv_proj[0], edge, gb, gate_proj[0], residual[0], out_weight, w_gate, w_up, w_down,
        live.astype(F32)[:, None], conv_weight, norm_gain[None], mlp_gain[None],
    )
    return hidden[None], state[None, None], edges[None, : CONV - 1]


def solution(mesh):
    return jax.shard_map(
        local_step,
        mesh=mesh,
        in_specs=(
            P("req", "seq", None),
            P("req", "seq", None),
            P("req", "seq", None),
            P("req", "seq", None),
            P("req", "seq", None),
            P(),
            P(),
            P(),
            P(),
            P(("req", "seq"), None),
            P(),
            P("req", "seq"),
            P("req", "seq"),
            P("seq", "req"),
        ),
        out_specs=(P("req", "seq", None), P("req", "seq", None, None), P("req", None, "seq")),
        check_vma=False,
    )
```

```python
import functools

import jax
import jax.numpy as jnp
from jax import lax
from jax.experimental import pallas as pl
from jax.experimental.pallas import tpu as pltpu
from jax.sharding import PartitionSpec as P

MESH = pl.DeviceIdType.MESH
BF = jnp.bfloat16
F32 = jnp.float32

HEADS = 8
DK = 128
DV = 256
CONV = 4
HK = 1024
PIECE = 128
D = 2048
UNITS = 704
HALF = UNITS // 2
PAD = 16
EPS_NORM = 1e-05
EPS_UNIT = 1e-06


def dot(a, b):
    return jnp.dot(a, b, preferred_element_type=F32)


def dot_nt(a, b):
    return lax.dot_general(a, b, (((1,), (1,)), ((), ())), preferred_element_type=F32)


def parts(a):
    high = a.astype(BF)
    return high, (a - high.astype(F32)).astype(BF)


def left3(a):
    high, low = parts(a)
    return jnp.concatenate([high, high, low], axis=1)


def right3(a, axis=0):
    high, low = parts(a)
    return jnp.concatenate([high, low, high], axis=axis)


def silu(v):
    return v / (1.0 + jnp.exp(-v))


class Copies:
    def __init__(self, send, recv):
        self.send, self.recv, self.used, self.sent = send, recv, 0, []

    def take(self):
        self.used += 1
        return self.used - 1

    def start(self, index, view, device, own=None):
        src, dst = (own if own is not None else view()), view()
        copy = pltpu.make_async_remote_copy(
            src_ref=src,
            dst_ref=dst,
            send_sem=self.send.at[index],
            recv_sem=self.recv.at[index],
            device_id=device,
            device_id_type=MESH,
        )
        copy.start()
        self.sent.append((index, view, device))

    def arrived(self, index, dst, device):
        pltpu.make_async_remote_copy(
            src_ref=dst,
            dst_ref=dst,
            send_sem=self.send.at[index],
            recv_sem=self.recv.at[index],
            device_id=device,
            device_id_type=MESH,
        ).wait_recv()

    def drain(self):
        for index, view, device in self.sent:
            src = dst = view()
            pltpu.make_async_remote_copy(
                src_ref=src,
                dst_ref=dst,
                send_sem=self.send.at[index],
                recv_sem=self.recv.at[index],
                device_id=device,
                device_id_type=MESH,
            ).wait_send()
        self.sent = []


class Ring:
    def __init__(self, copies, me, plus, minus, items):
        self.copies, self.me, self.plus, self.minus = copies, me, plus, minus
        self.items = [(own, slot, half, [copies.take() for _ in range(4)]) for own, slot, half in items]
        self.left, self.right, self.far = (lax.rem(me + step, 4) for step in (3, 1, 2))

    def first(self):
        for own, slot, half, sems in self.items:
            view = functools.partial(slot, self.me)
            self.copies.start(sems[0], view, self.plus, own)
            self.copies.start(sems[1], view, self.minus, own)

    def second(self):
        for own, slot, half, sems in self.items:
            left, right = self.left, self.right
            self.copies.arrived(sems[0], slot(left), self.plus)
            self.copies.start(sems[2], functools.partial(half, left, 0), self.plus)
            self.copies.arrived(sems[1], slot(right), self.minus)
            self.copies.start(sems[3], functools.partial(half, right, 1), self.minus)

    def last(self):
        for own, slot, half, sems in self.items:
            far = self.far
            self.copies.arrived(sems[2], half(far, 0), self.plus)
            self.copies.arrived(sems[3], half(far, 1), self.minus)


def body(
    qkv, edge_in, gb_in, gate_in, res_in, out_w, w_gate, w_up, w_down,
    live, conv_w, norm_gain, mlp_gain,
    hidden, state_out, edge_out,
    kbuf, vbuf, qbuf, gbuf, ebuf,
    x3, kn_s, tv_s, tk_s, kd_s, a_s, qe_s, dec_s, w_s,
    obuf, mixed, gate, resid, stream,
    ow, wg, wu, wd, tok,
    hbuf, pown, psib, prec, s2, sn, r2, rn,
    send, recv, asend, arecv, bsend, brecv, local,
):
    req = lax.axis_index("req")
    seq = lax.axis_index("seq")
    y, x = lax.div(req, 4), lax.rem(req, 4)
    z, c = lax.div(seq, 2), lax.rem(seq, 2)
    other = 1 - c

    def up(v):
        return lax.rem(v + 1, 4)

    def down(v):
        return lax.rem(v + 3, 4)

    xu, xd, xf = up(x), down(x), lax.rem(x + 2, 4)
    yu, yd, yf = up(y), down(y), lax.rem(y + 2, 4)
    zu, zd, zf = up(z), down(z), lax.rem(z + 2, 4)
    xp, xm = (y * 4 + up(x), seq), (y * 4 + down(x), seq)
    yp, ym = (up(y) * 4 + x, seq), (down(y) * 4 + x, seq)
    zp, zm = (req, up(z) * 2 + c), (req, down(z) * 2 + c)
    sib = (req, z * 2 + other)

    barrier = pltpu.get_barrier_semaphore()
    for dev in (xp, xm, yp, ym):
        pl.semaphore_signal(barrier, inc=1, device_id=dev, device_id_type=MESH)
    for step in range(1, 8):
        pl.semaphore_signal(
            barrier, inc=1, device_id=(req, lax.rem(seq + step, 8)), device_id_type=MESH
        )

    def near(index, src, dst):
        return pltpu.make_async_copy(src, dst, local.at[index])

    qcol = pl.multiple_of(seq * DK, DK)
    kcol = pl.multiple_of(HK + seq * DK, DK)
    vcol = pl.multiple_of(2 * HK + seq * DV, DV)
    mine = pl.ds(pl.multiple_of(PAD + seq * PIECE, 16), PIECE)
    locals_ = [
        near(0, gb_in.at[seq], gbuf.at[seq]),
        near(1, qkv.at[:, pl.ds(kcol, DK)], kbuf.at[mine]),
        near(2, qkv.at[:, pl.ds(vcol, DV)], vbuf.at[mine]),
        near(3, qkv.at[:, pl.ds(qcol, DK)], qbuf.at[mine]),
        near(4, edge_in.at[seq], ebuf.at[seq]),
        near(5, gate_in, gate),
        near(6, res_in, resid),
        near(7, out_w, ow.at[y, x, z, c]),
        near(8, w_gate, wg.at[y, x]),
        near(9, w_up, wu.at[y, x]),
        near(10, w_down, wd.at[y, x]),
    ]
    for copy in locals_:
        copy.start()
    for buf in (kbuf, vbuf, qbuf):
        buf[0:PAD, :] = jnp.zeros((PAD, buf.shape[1]), BF)
    pl.semaphore_wait(barrier, 11)

    copies = Copies(send, recv)

    def cut(ref, first, size):
        return ref.at[pl.ds(first, size)]

    ring_oz = Ring(copies, z, zp, zm, [(
        out_w,
        lambda i: ow.at[y, x, i, c],
        lambda i, h: ow.at[y, x, i, c, :, h * 1024 : h * 1024 + 1024],
    )])
    ring_wax = Ring(copies, x, xp, xm, [
        (w_gate, lambda i: wg.at[y, i], lambda i, h: wg.at[y, i, h * 64 : h * 64 + 64]),
        (
            w_down.at[0:HALF],
            lambda i: wd.at[y, i, 0:HALF],
            lambda i, h: wd.at[y, i, h * 176 : h * 176 + 176],
        ),
    ])
    ring_wby = Ring(copies, y, yp, ym, [
        (w_up, lambda i: wu.at[i, x], lambda i, h: wu.at[i, x, h * 64 : h * 64 + 64]),
        (
            w_down.at[HALF:UNITS],
            lambda i: wd.at[i, x, HALF:UNITS],
            lambda i, h: wd.at[i, x, HALF + h * 176 : HALF + h * 176 + 176],
        ),
    ])
    ring_way = Ring(copies, y, yp, ym, [
        (None, lambda i: wg.at[i], lambda i, h: wg.at[i, 2 * h : 2 * h + 2]),
        (None, lambda i: wd.at[i, :, 0:HALF], lambda i, h: wd.at[i, 2 * h : 2 * h + 2, 0:HALF]),
    ])
    ring_wbx = Ring(copies, x, xp, xm, [
        (None, lambda i: wu.at[:, i], lambda i, h: wu.at[2 * h : 2 * h + 2, i]),
        (
            None,
            lambda i: wd.at[:, i, HALF:UNITS],
            lambda i, h: wd.at[2 * h : 2 * h + 2, i, HALF:UNITS],
        ),
    ])
    lo, hi = slice(0, 1024), slice(1024, 2048)
    ring_o1x = Ring(copies, x, xp, xm, [(
        None,
        lambda i: ow.at[y, i, :, c, :, lo],
        lambda i, h: ow.at[y, i, 2 * h : 2 * h + 2, c, :, lo],
    )])
    ring_o2y = Ring(copies, y, yp, ym, [(
        None,
        lambda i: ow.at[i, x, :, c, :, hi],
        lambda i, h: ow.at[i, x, 2 * h : 2 * h + 2, c, :, hi],
    )])
    ring_o1y = Ring(copies, y, yp, ym, [(
        None,
        lambda i: ow.at[i, :, :, c, :, lo],
        lambda i, h: ow.at[i, 2 * h : 2 * h + 2, :, c, :, lo],
    )])
    ring_o2x = Ring(copies, x, xp, xm, [(
        None,
        lambda i: ow.at[:, i, :, c, :, hi],
        lambda i, h: ow.at[2 * h : 2 * h + 2, i, :, c, :, hi],
    )])
    ring_tok = Ring(copies, z, zp, zm, [(
        None,
        lambda i: tok.at[i, c],
        lambda i, h: tok.at[i, c, h * 64 : h * 64 + 64],
    )])

    def exchange(kind, src, dst, dev, peer):
        return pltpu.make_async_remote_copy(
            src_ref=src, dst_ref=dst, send_sem=asend.at[kind, peer], recv_sem=arecv.at[kind, seq],
            device_id=dev, device_id_type=MESH,
        )

    def views(kind, head, piece):
        rows = pl.ds(pl.multiple_of(PAD + piece * PIECE, 16), PIECE)
        if kind == 0:
            return gb_in.at[head], gbuf.at[piece]
        if kind == 1:
            return qkv.at[:, pl.ds(pl.multiple_of(HK + head * DK, DK), DK)], kbuf.at[rows]
        if kind == 2:
            return qkv.at[:, pl.ds(pl.multiple_of(2 * HK + head * DV, DV), DV)], vbuf.at[rows]
        if kind == 3:
            return qkv.at[:, pl.ds(pl.multiple_of(head * DK, DK), DK)], qbuf.at[rows]
        return edge_in.at[head], ebuf.at[piece]

    order = (4, 3, 5, 2, 6, 7, 1)

    def spread(kind):
        for step in order:
            peer = lax.rem(seq + step, 8)
            src, dst = views(kind, peer, seq)
            exchange(kind, src, dst, (req, peer), peer).start()

    def piece_arrived(kind, piece):
        @pl.when(piece != seq)
        def _():
            src, dst = views(kind, seq, piece)
            pltpu.make_async_remote_copy(
                src_ref=dst, dst_ref=dst, send_sem=asend.at[kind, piece],
                recv_sem=arecv.at[kind, piece], device_id=(req, piece), device_id_type=MESH,
            ).wait_recv()

    ring_oz.first()
    spread(0)
    spread(1)
    ring_wax.first()
    ring_wby.first()
    ring_oz.second()
    spread(2)
    spread(3)
    spread(4)
    for index in range(4):
        locals_[index].wait()

    row = lax.broadcasted_iota(jnp.int32, (PIECE, PIECE), 0)
    col = lax.broadcasted_iota(jnp.int32, (PIECE, PIECE), 1)

    def convolve(buf, piece, taps):
        window = buf[pl.ds(pl.multiple_of(piece * PIECE, 16), PAD + PIECE), :].astype(F32)
        total = window[PAD:] * taps[CONV - 1 : CONV]
        for tap in range(CONV - 1):
            total = total + pltpu.roll(window, CONV - 1 - tap, 0)[PAD:] * taps[tap : tap + 1]
        return silu(total)

    def unit(v):
        return v * lax.rsqrt(jnp.sum(v * v, axis=-1, keepdims=True) + EPS_UNIT)

    def gates(piece):
        tile = gbuf[piece]
        log_row, beta_row = tile[0:1], tile[1:2]
        grown = jnp.sum(jnp.where(col <= row, log_row, 0.0), axis=1, keepdims=True)
        beta = jnp.sum(jnp.where(col == row, beta_row, 0.0), axis=1, keepdims=True)
        return log_row, grown, beta

    ktaps = conv_w[:, pl.ds(kcol, DK)]
    vtaps = conv_w[:, pl.ds(vcol, DV)]
    qtaps = conv_w[:, pl.ds(qcol, DK)]
    eye = jnp.where(row == col, 1.0, 0.0).astype(F32)

    GROUP = 4

    def invert(step, carry):
        pieces = [step * GROUP + j for j in range(GROUP)]
        for piece in pieces:
            piece_arrived(0, piece)
            piece_arrived(1, piece)
        couples, inverses = [], []
        for piece in pieces:
            key = unit(convolve(kbuf, piece, ktaps))
            kn_s[piece] = key
            log_row, grown, beta = gates(piece)
            log_col = jnp.sum(jnp.where(col == row, log_row, 0.0), axis=1, keepdims=True)
            along = jnp.sum(jnp.where(row <= col, log_col, 0.0), axis=0, keepdims=True)
            within = jnp.where(col <= row, jnp.exp(jnp.minimum(grown - along, 0.0)), 0.0)
            w_s[piece] = within
            inner = dot_nt(left3(key), right3(key, 1))
            couple = jnp.where(col < row, beta * within * inner, 0.0)
            couples.append(couple)
            inverses.append(eye - jnp.where((row // 2) == (col // 2), couple, 0.0))
        size = 2
        while size < PIECE:
            mask = ((row // (2 * size)) == (col // (2 * size))) & ((row // size) != (col // size))
            lows = [v.astype(BF) for v in inverses]
            mids = [
                dot(low, jnp.where(mask, couple, 0.0).astype(BF)).astype(BF)
                for low, couple in zip(lows, couples)
            ]
            inverses = [v - dot(mid, low) for v, mid, low in zip(inverses, mids, lows)]
            size *= 2
        rests = [
            eye - v - dot(left3(couple), right3(v)) for v, couple in zip(inverses, couples)
        ]
        for piece, v, rest in zip(pieces, inverses, rests):
            x3[piece] = left3(v + dot(v.astype(BF), rest.astype(BF)))

        @pl.when(step == 0)
        def _():
            ring_oz.last()
            locals_[7].wait()
            ring_o1x.first()
            ring_o2y.first()
            ring_wax.second()
            ring_wby.second()

        return carry

    lax.fori_loop(0, HEADS // GROUP, invert, 0)
    ring_o1x.second()
    ring_o2y.second()

    forwards = [copies.take() for _ in range(8)]

    def forward_o(first, index):
        copies.start(forwards[first], lambda: ow.at[index[0], :, :, c, :, lo], sib)
        copies.start(forwards[first + 1], lambda: ow.at[:, index[1], :, c, :, hi], sib)

    def prepare(step, carry):
        pieces = [step * 2 + j for j in range(2)]
        for piece in pieces:
            piece_arrived(2, piece)
            piece_arrived(3, piece)
        for piece in pieces:
            query = unit(convolve(qbuf, piece, qtaps)) * DK ** (-0.5)
            value = convolve(vbuf, piece, vtaps)
            key = kn_s[piece]
            log_row, grown, beta = gates(piece)
            whole = jnp.sum(log_row, axis=1, keepdims=True)
            growth = jnp.exp(grown)
            a_s[piece] = (w_s[piece] * dot_nt(left3(query), right3(key, 1))).astype(BF)
            qe_s[piece] = (growth * query).astype(BF)
            both = jnp.concatenate([beta * value, (beta * growth) * key], axis=1)
            solved = dot(x3[piece], right3(both))
            tv_s[piece] = solved[:, :DV]
            tk_s[piece] = left3(solved[:, DV:])
            kd_s[piece] = left3(jnp.transpose(jnp.exp(jnp.minimum(whole - grown, 0.0)) * key))
            dec_s[piece] = jnp.broadcast_to(jnp.exp(whole), (8, DV))

        @pl.when(step == 1)
        def _():
            ring_o1x.last()
            ring_o2y.last()
            ring_o1y.first()
            ring_o2x.first()
            forward_o(0, (y, x))

        return carry

    lax.fori_loop(0, HEADS // 2, prepare, 0)

    for index in (8, 9, 10):
        locals_[index].wait()
    ring_wax.last()
    ring_wby.last()
    ring_way.first()
    ring_wbx.first()

    state_out[...] = jnp.zeros((DK, DV), F32)

    def back(piece):
        return pltpu.make_async_remote_copy(
            src_ref=obuf.at[piece], dst_ref=mixed.at[seq], send_sem=bsend.at[piece],
            recv_sem=brecv.at[seq], device_id=(req, piece), device_id_type=MESH,
        )

    def serial(piece, carry):
        running = state_out[...]
        corrected = tv_s[piece] - dot(tk_s[piece], right3(running))
        result = dot(qe_s[piece], running.astype(BF)) + dot(a_s[piece], corrected.astype(BF))
        state_out[...] = dec_s[piece][0:1] * running + dot(kd_s[piece], right3(corrected))
        scaled = result * lax.rsqrt(jnp.mean(result * result, axis=-1, keepdims=True) + EPS_NORM)

        @pl.when(piece == seq)
        def _():
            mixed[seq] = scaled.astype(BF)

        @pl.when(piece != seq)
        def _():
            obuf[piece] = scaled.astype(BF)
            back(piece).start()

        @pl.when(piece == 3)
        def _():
            ring_o1y.second()
            ring_o2x.second()
            forward_o(2, (yd, xd))
            forward_o(4, (yu, xu))

        return carry

    lax.fori_loop(0, HEADS, serial, 0)

    for index in (5, 6):
        locals_[index].wait()

    ring_o1y.last()
    ring_o2x.last()
    forward_o(6, (yf, xf))

    for head in range(HEADS):
        @pl.when(head != seq)
        def _():
            pltpu.make_async_remote_copy(
                src_ref=mixed.at[head], dst_ref=mixed.at[head], send_sem=bsend.at[head],
                recv_sem=brecv.at[head], device_id=(req, head), device_id_type=MESH,
            ).wait_recv()

    gain = norm_gain[...]

    def gated(head, carry):
        columns = pl.ds(pl.multiple_of(head * DV, DV), DV)
        value = silu(gate[:, columns].astype(F32)) * gain
        mixed[head] = (mixed[head].astype(F32) * value).astype(BF)
        return carry

    lax.fori_loop(0, HEADS, gated, 0)

    for first, pair in ((0, (y, x)), (2, (yd, xd)), (4, (yu, xu)),
                        (6, (yf, xf))):
        copies.arrived(forwards[first], ow.at[pair[0], :, :, other, :, lo], sib)
        copies.arrived(forwards[first + 1], ow.at[:, pair[1], :, other, :, hi], sib)

    def project(tile, squares):
        columns = pl.ds(pl.multiple_of(tile * 256, 256), 256)
        attended = jnp.zeros((PIECE, 256), F32)
        for head in range(HEADS):
            rows = ow[head // 2, 2 * (head % 2) : 2 * (head % 2) + 2, :, :, :, columns]
            attended = attended + dot(mixed[head], rows.reshape(DV, 256))
        summed = (resid[:, columns].astype(F32) + attended).astype(BF)
        stream[:, columns] = summed
        wide = summed.astype(F32)
        return squares + jnp.sum(wide * wide, axis=-1, keepdims=True)

    squares = lax.fori_loop(0, D // 256, project, jnp.zeros((PIECE, 1), F32))
    scale = lax.rsqrt(squares * (1.0 / D) + EPS_NORM)
    tok[z, c] = (stream[...].astype(F32) * scale * mlp_gain[...]).astype(BF)

    tok_forward = [copies.take() for _ in range(4)]
    ring_tok.first()

    def forward_tok(index, zi):
        copies.start(tok_forward[index], lambda: tok.at[zi, c], sib)

    forward_tok(0, z)
    ring_tok.second()
    forward_tok(1, zd)
    forward_tok(2, zu)

    ring_way.second()
    ring_wbx.second()
    ring_tok.last()
    forward_tok(3, zf)
    for index, zi in ((0, z), (1, zd), (2, zu), (3, zf)):
        copies.arrived(tok_forward[index], tok.at[zi, other], sib)
    ring_way.last()
    ring_wbx.last()

    half_ids = [copies.take() for _ in range(4)]

    def cross(zi):
        return pltpu.make_async_remote_copy(
            src_ref=psib.at[zi], dst_ref=prec.at[zi], send_sem=bsend.at[8 + zi],
            recv_sem=brecv.at[8 + zi], device_id=sib, device_id_type=MESH,
        )

    def paired(zi):
        cross(zi).wait_recv()
        return pown[zi] + prec[zi].astype(F32)

    def far_sum():
        s2[...] = paired(zf).astype(BF)
        copies.start(half_ids[0], lambda: r2.at[0], zp, s2.at[0:64])
        copies.start(half_ids[1], lambda: r2.at[1], zm, s2.at[64:128])

    def next_sum(index):
        total = paired(zu if index == 0 else zd)
        copies.arrived(half_ids[index], r2.at[index], zp if index == 0 else zm)
        other_half = r2[index].astype(F32)
        if index == 0:
            sn[0, 0:64] = (total[0:64] + other_half).astype(BF)
            sn[0, 64:128] = total[64:128].astype(BF)
        else:
            sn[1, 0:64] = total[0:64].astype(BF)
            sn[1, 64:128] = (total[64:128] + other_half).astype(BF)
        copies.start(half_ids[2 + index], lambda: rn.at[index], zp if index == 0 else zm, sn.at[index])

    def ffn(step, carry):
        zi = (z + 10 - (step * (step + 1)) // 2) % 4
        tokens = jnp.concatenate([tok[zi, c], tok[zi, other]], axis=0)
        for first, width in ((0, 256), (256, 256), (512, 192)):
            gate_w = wg[:, :, :, first : first + width].reshape(D, width)
            up_w = wu[:, :, :, first : first + width].reshape(D, width)
            inner = silu(dot(tokens, gate_w)) * dot(tokens, up_w)
            hbuf[:, first : first + width] = inner.astype(BF)

        def lower(tile, carry):
            yi, xi = tile // 2, 2 * (tile % 2)
            rows = jnp.concatenate([wd[yi, xi], wd[yi, xi + 1]], axis=1)
            result = dot(hbuf[...], rows)
            columns = pl.ds(pl.multiple_of(tile * 256, 256), 256)
            pown[zi, :, columns] = result[:PIECE]
            psib[zi, :, columns] = result[PIECE:].astype(BF)
            return carry

        lax.fori_loop(0, D // 256, lower, 0)
        cross(zi).start()

        @pl.when(step == 1)
        def _():
            far_sum()

        @pl.when(step == 2)
        def _():
            next_sum(0)

        @pl.when(step == 3)
        def _():
            next_sum(1)

        return carry

    lax.fori_loop(0, 4, ffn, 0)

    total = stream[...].astype(F32) + paired(z)
    copies.arrived(half_ids[2], rn.at[0], zp)
    copies.arrived(half_ids[3], rn.at[1], zm)
    total = total + rn[0].astype(F32) + rn[1].astype(F32)
    hidden[...] = (total * live[...]).astype(BF)

    for piece in range(HEADS):
        piece_arrived(4, piece)
    locals_[4].wait()
    edges = ebuf[0].astype(F32)
    for piece in range(1, HEADS):
        edges = edges + ebuf[piece].astype(F32)
    edge_out[...] = edges.astype(BF)

    copies.drain()
    for kind in range(5):
        for step in order:
            peer = lax.rem(seq + step, 8)
            src, dst = views(kind, peer, seq)
            exchange(kind, src, dst, (req, peer), peer).wait_send()
    for step in range(1, 8):
        back(lax.rem(seq + step, 8)).wait_send()
    for zi in range(4):
        cross(zi).wait_send()


def layer(qkv, edge, gb, gate, residual, out_weight, w_gate, w_up, w_down, live, conv_weight, norm_gain, mlp_gain):
    hbm = pl.BlockSpec(memory_space=pl.ANY)
    vmem = pl.BlockSpec(memory_space=pltpu.VMEM)
    n_sems = 96
    scratch = [
        pltpu.VMEM((PAD + 1024, DK), BF),
        pltpu.VMEM((PAD + 1024, DV), BF),
        pltpu.VMEM((PAD + 1024, DK), BF),
        pltpu.VMEM((8, 8, 128), F32),
        pltpu.VMEM((8, 16, 512), BF),
        pltpu.VMEM((8, 128, 384), BF),
        pltpu.VMEM((8, 128, 128), F32),
        pltpu.VMEM((8, 128, 256), F32),
        pltpu.VMEM((8, 128, 384), BF),
        pltpu.VMEM((8, 128, 384), BF),
        pltpu.VMEM((8, 128, 128), BF),
        pltpu.VMEM((8, 128, 128), BF),
        pltpu.VMEM((8, 8, 256), F32),
        pltpu.VMEM((8, 128, 128), F32),
        pltpu.VMEM((8, 128, 256), BF),
        pltpu.VMEM((8, 128, 256), BF),
        pltpu.VMEM((128, 2048), BF),
        pltpu.VMEM((128, 2048), BF),
        pltpu.VMEM((128, 2048), BF),
        pltpu.VMEM((4, 4, 4, 2, 16, 2048), BF),
        pltpu.VMEM((4, 4, 128, UNITS), BF),
        pltpu.VMEM((4, 4, 128, UNITS), BF),
        pltpu.VMEM((4, 4, UNITS, 128), BF),
        pltpu.VMEM((4, 2, 128, 2048), BF),
        pltpu.VMEM((256, UNITS), BF),
        pltpu.VMEM((4, 128, 2048), F32),
        pltpu.VMEM((4, 128, 2048), BF),
        pltpu.VMEM((4, 128, 2048), BF),
        pltpu.VMEM((128, 2048), BF),
        pltpu.VMEM((2, 128, 2048), BF),
        pltpu.VMEM((2, 64, 2048), BF),
        pltpu.VMEM((2, 128, 2048), BF),
        pltpu.SemaphoreType.DMA((n_sems,)),
        pltpu.SemaphoreType.DMA((n_sems,)),
        pltpu.SemaphoreType.DMA((5, 8)),
        pltpu.SemaphoreType.DMA((5, 8)),
        pltpu.SemaphoreType.DMA((12,)),
        pltpu.SemaphoreType.DMA((12,)),
        pltpu.SemaphoreType.DMA((11,)),
    ]
    return pl.pallas_call(
        body,
        out_shape=(
            jax.ShapeDtypeStruct((PIECE, D), BF),
            jax.ShapeDtypeStruct((DK, DV), F32),
            jax.ShapeDtypeStruct((16, 512), BF),
        ),
        in_specs=[hbm] * 9 + [vmem] * 4,
        out_specs=(vmem, vmem, vmem),
        scratch_shapes=scratch,
        compiler_params=pltpu.CompilerParams(
            collective_id=0, has_side_effects=True, vmem_limit_bytes=64_000_000
        ),
        name="layer",
    )(qkv, edge, gb, gate, residual, out_weight, w_gate, w_up, w_down, live, conv_weight, norm_gain, mlp_gain)


def local_step(
    qkv_proj, gate_proj, residual, log_decay, beta_logit, lengths, slot_request, conv_weight,
    norm_gain, out_weight, mlp_gain, w_gate, w_up, w_down,
):
    seq_index = lax.axis_index("seq")
    req_index = lax.axis_index("req")
    ids = jnp.arange(slot_request.shape[0], dtype=jnp.int32)
    request = jnp.sum(jnp.where(ids == req_index, slot_request, 0))
    length = jnp.sum(jnp.where(ids == request, lengths, 0))
    position = seq_index * PIECE + jnp.arange(PIECE, dtype=jnp.int32)
    live = position < length
    beta = jax.nn.sigmoid(beta_logit[0].astype(F32)) * live[:, None]
    decay = jnp.where(live[:, None], log_decay[0], 0.0)
    gb = jnp.concatenate(
        [decay.T[:, None], beta.T[:, None], jnp.zeros((HEADS, 6, PIECE), F32)], axis=1
    )
    targets = length - (CONV - 1) + jnp.arange(16, dtype=jnp.int32)
    select = (position[None, :] == targets[:, None]) & (jnp.arange(16)[:, None] < CONV - 1)
    edge = jnp.dot(select.astype(BF), qkv_proj[0], preferred_element_type=F32).astype(BF)
    edge = edge.reshape(16, 8, 512).transpose(1, 0, 2)
    hidden, state, edges = layer(
        qkv_proj[0], edge, gb, gate_proj[0], residual[0], out_weight, w_gate, w_up, w_down,
        live.astype(F32)[:, None], conv_weight, norm_gain[None], mlp_gain[None],
    )
    return hidden[None], state[None, None], edges[None, : CONV - 1]


def solution(mesh):
    return jax.shard_map(
        local_step,
        mesh=mesh,
        in_specs=(
            P("req", "seq", None),
            P("req", "seq", None),
            P("req", "seq", None),
            P("req", "seq", None),
            P("req", "seq", None),
            P(),
            P(),
            P(),
            P(),
            P(("req", "seq"), None),
            P(),
            P("req", "seq"),
            P("req", "seq"),
            P("seq", "req"),
        ),
        out_specs=(P("req", "seq", None), P("req", "seq", None, None), P("req", None, "seq")),
        check_vma=False,
    )
```
